32 devices in a mesh: hyp: 2 (over y), row: 4 (over z), col: 4 (over x, core).
Axes of the slice: x: 2, y: 2, z: 4, core: 2. Of those that a mesh axis runs over, the one named last changes fastest.
Arguments:
- inverse_tile: float32 [16384, 8192], P(('hyp', 'row'), 'col'), parts along dimension 0, may hold values from -32768 to 262144, as said below
- panels: float32 [2, 2, 8192, 512], P('hyp', None, ('col', 'row')), parts along dimension 0, may hold values from -0.0007324219 to 0.0007324219
- link_panel: float32 [2, 512, 512], P('hyp'), parts along dimension 0, may hold values from -0.09375 to 0.09375
- diag_inverse: float32 [2, 2, 512, 512], P('hyp', None, 'row', 'col'), parts along dimension 0, may hold values from -3 to 3
- ancestor_tiles: int32 [1, 2, 64], replicated, may hold values 0 or 1
Outputs:
- ancestor_block: float32 [2, 2, 8192, 512], P('hyp', None, ('row', 'col')), parts along dimension 0
- diag_block: float32 [2, 2, 512, 512], P('hyp', None, 'row', 'col'), parts along dimension 0
- cross_block: float32 [2, 512, 512], P('hyp', 'row', 'col'), parts along dimension 0
The draws below stay inside these ranges and needn't reach their ends.
There are 2 independent parts, one for each index of `hyp`. The reference program is written for one: setup_inputs(seed, part) draws one part's arguments, and reference() takes and returns one part's arrays. A program takes and returns all parts, laid end to end along the dimension named above; an argument that names none is the same for every part. Nothing has to cross between parts.
Inputs may be any that keep to these rules, and one draw needn't show every extreme that they name: `inverse_tile`: symmetric.
All inputs are finite; a program needn't handle non-finite values.
Results may differ from the reference program's by a relative error of at most 0.000075.
Values sent between devices are 32-bit elements; how exact they have to be, the bound alone decides.
A program may use at most 128 MiB of HBM per device.

```python
import jax
import jax.numpy as jnp
from jax import lax

ANC = 8192
B = 512
TILE = 128
SIB = 1
TILES = 64


def draw_inverse_tile(key, part):
    noise_key = jax.random.fold_in(key, 11)
    diag_key = jax.random.fold_in(key, 23)
    noise = jax.random.normal(noise_key, (ANC, ANC), jnp.float32)
    spread = 0.35 * jnp.sqrt(jnp.float32(ANC))
    symmetric = (noise + noise.T) * spread
    diagonal = jax.random.uniform(diag_key, (ANC,), jnp.float32, 1.0, 2.0) * ANC
    matrix = symmetric + jnp.diag(diagonal - jnp.diagonal(symmetric))
    return matrix


def with_ends(values, rng, low, top_value):
    longest = values.shape.index(max(values.shape))
    spots = []
    for shift in (0, 1):
        where = [jax.random.randint(jax.random.fold_in(rng, axis), (), 0, length) for axis, length in enumerate(values.shape)]
        where[longest] = (where[longest] + shift) % values.shape[longest]
        spots.append(tuple(where))
    return values.at[spots[0]].set(low).at[spots[1]].set(top_value)


def shard_levels(stream_key, dims, split, smallest, top_value):
    level = 1.0
    for position, blocks in split:
        steps = jax.random.uniform(jax.random.fold_in(jax.random.fold_in(stream_key, 6), position), (blocks,), jnp.float32, smallest / len(split), top_value / len(split))
        level = level * jnp.repeat(jnp.exp(steps), dims[position] // blocks).reshape((-1,) + (1,) * (len(dims) - 1 - position))
    return level


def normal_values(key, shape, deviation, bound, shards=(), dtype=jnp.bfloat16):
    entries = jax.random.normal(key, shape, jnp.float32) * deviation
    if len(shards) > 0:
        entries = shard_levels(key, shape, shards, -0.22, 0.18) * entries
    return jnp.clip(entries, min=-bound, max=bound).astype(dtype)


def setup_inputs(seed: int = 0, part: int = 0) -> dict:
    seeds = jax.random.split(jax.random.key(seed), 6)
    own_keys = jax.random.split(jax.random.fold_in(seeds[5], part), 6)
    return {
        "inverse_tile": draw_inverse_tile(jax.random.fold_in(jax.random.fold_in(seeds[5], part), 71), part),
        "panels": normal_values(own_keys[1], (SIB, 2, ANC, B), (ANC * ANC) ** -0.5, 0.0007324219, ((2, 16),), jnp.float32),
        "link_panel": normal_values(own_keys[2], (SIB, B, B), (8 * B) ** -0.5, 0.09375, (), jnp.float32),
        "diag_inverse": normal_values(own_keys[3], (SIB, 2, B, B), 0.5, 3.0, ((2, 4), (3, 4)), jnp.float32),
        "ancestor_tiles": with_ends((jax.random.randint(seeds[4], (SIB, 2, TILES), 0, 4) < 3).astype(jnp.int32), jax.random.fold_in(seeds[4], 1), 0, 1),
    }


def reference(inverse_tile, panels, link_panel, diag_inverse, ancestor_tiles):
    precise = lax.Precision.HIGHEST
    rows_kept = jnp.repeat(ancestor_tiles, TILE, axis=2).astype(jnp.float32)
    masked = panels * rows_kept[..., None]
    first = masked[:, 0]
    second = masked[:, 1]
    ancestor_first = -jnp.einsum("ik,skb->sib", inverse_tile, first, precision=precise)
    diag_first = diag_inverse[:, 0] - jnp.einsum("sib,sic->sbc", first, ancestor_first, precision=precise)
    ancestor_second = -(jnp.einsum("ik,skb->sib", inverse_tile, second, precision=precise)
                        + jnp.einsum("sik,skc->sic", ancestor_first, link_panel, precision=precise))
    cross_block = -(jnp.einsum("sib,sic->sbc", ancestor_first, second, precision=precise)
                    + jnp.einsum("sbk,skc->sbc", diag_first, link_panel, precision=precise))
    diag_second = (diag_inverse[:, 1]
                   - jnp.einsum("sib,sic->sbc", second, ancestor_second, precision=precise)
                   - jnp.einsum("skb,skc->sbc", link_panel, cross_block, precision=precise))
    ancestor_block = jnp.stack([ancestor_first, ancestor_second], axis=1)
    diag_block = jnp.stack([diag_first, diag_second], axis=1)
    return ancestor_block, diag_block, cross_block
```

```python
import jax
import jax.numpy as jnp
from jax import lax
from jax.sharding import PartitionSpec as P

TILE = 128

precise = lax.Precision.HIGH
fine = lax.Precision.HIGHEST


def dot(a, b, contract, precision=precise):
    return lax.dot_general(a, b, ((contract[0:1], contract[1:2]), ((), ())), precision=precision)


def mask_panels(panels, ancestor_tiles):
    rows_axis = lax.axis_size("row")
    local_rows = panels.shape[2]
    row_start = (lax.axis_index("col") * rows_axis + lax.axis_index("row")) * local_rows
    tile_mask = jnp.repeat(ancestor_tiles, TILE, axis=2)
    kept_rows = lax.dynamic_slice_in_dim(tile_mask, row_start, local_rows, 2)
    return jnp.where(kept_rows[..., None] != 0, panels, 0.0)


def own_panels(masked):
    rows_axis, cols_axis = lax.axis_size("row"), lax.axis_size("col")
    pairs = []
    for r in range(rows_axis):
        for c in range(cols_axis):
            block = r * cols_axis + c
            pairs.append(((block % rows_axis) * cols_axis + block // rows_axis, block))
    return lax.ppermute(masked, ("row", "col"), pairs)


def finish(y, own, link, diag_inverse):
    row_id = lax.axis_index("row")
    col_id = lax.axis_index("col")
    height, span = diag_inverse.shape[1:]
    first, second = own[0], own[1]
    y1 = -y[0]
    y2 = -(y[1] + dot(y1, link, (1, 0)))
    shifted = second - dot(first, link, (1, 0))
    link_rows = lax.dynamic_slice_in_dim(link, row_id * height, height, 0)
    link_cols = lax.dynamic_slice_in_dim(link, col_id * span, span, 0)
    given = dot(diag_inverse[0], link_cols, (1, 0))
    f1 = dot(first, y1, (0, 0))
    f2 = dot(first, y2, (0, 0))
    f2 = lax.dynamic_update_slice_in_dim(
        f2, lax.dynamic_slice_in_dim(f2, row_id * height, height, 0) + given, row_id * height, 0
    )
    s2 = dot(shifted, y2, (0, 0)) - dot(link_rows, given, (0, 0))
    terms = jnp.stack([f1, f2, s2])
    terms = lax.psum_scatter(terms, "row", scatter_dimension=1, tiled=True)
    terms = lax.psum_scatter(terms, "col", scatter_dimension=2, tiled=True)
    diag = jnp.stack([diag_inverse[0] - terms[0], diag_inverse[1] - terms[2]])
    return jnp.stack([y1, y2]), diag, -terms[1]


def local(inverse_tile, panels, link_panel, diag_inverse, ancestor_tiles):
    masked = mask_panels(panels, ancestor_tiles)[0]
    own = own_panels(masked)
    ys = []
    for k in range(2):
        full = lax.all_gather(masked[k], "row", axis=0, tiled=True)
        ys.append(lax.psum_scatter(dot(inverse_tile, full, (1, 0)), "col", scatter_dimension=0, tiled=True))
    anc, diag, cross = finish(jnp.stack(ys), own, link_panel[0], diag_inverse[0])
    return anc[None], diag[None], cross[None]


def solution(mesh):
    in_specs = (
        P(("hyp", "row"), "col"),
        P("hyp", None, ("col", "row"), None),
        P("hyp", None, None),
        P("hyp", None, "row", "col"),
        P(),
    )
    out_specs = (
        P("hyp", None, ("row", "col"), None),
        P("hyp", None, "row", "col"),
        P("hyp", "row", "col"),
    )
    return jax.shard_map(local, mesh=mesh, in_specs=in_specs, out_specs=out_specs, check_vma=False)
```

```python
import functools

import jax
import jax.numpy as jnp
from jax import lax
from jax.experimental import pallas as pl
from jax.experimental.pallas import tpu as pltpu
from jax.sharding import PartitionSpec as P

TILE = 128
MESH = pl.DeviceIdType.MESH

precise = lax.Precision.HIGH


def dot(a, b, contract, precision=precise):
    return lax.dot_general(a, b, ((contract[0:1], contract[1:2]), ((), ())), precision=precision)


def mask_panels(panels, ancestor_tiles):
    rows_axis = lax.axis_size("row")
    local_rows = panels.shape[2]
    row_start = (lax.axis_index("col") * rows_axis + lax.axis_index("row")) * local_rows
    tile_mask = jnp.repeat(ancestor_tiles, TILE, axis=2)
    kept_rows = lax.dynamic_slice_in_dim(tile_mask, row_start, local_rows, 2)
    return jnp.where(kept_rows[..., None] != 0, panels, 0.0)


def exchange(axis_sizes, chunks, a_hbm, x_hbm, y_ref, own_ref, a_hi, a_lo, stage, p_hi, p_lo, gathered, partial,
             received, own, stage_sem, load_sem, send_sem, recv_sem, part_send, part_recv, own_send, own_recv, own_local):
    rows_axis, cols_axis = axis_sizes
    r = lax.axis_index("row")
    c = lax.axis_index("col")
    _, _, rows, width = gathered.shape
    half = rows // 2
    per_panel = chunks // x_hbm.shape[0]
    pieces = 2 * (rows_axis - 1)
    tile = stage.shape[1]
    tiles = a_hbm.shape[0] // tile

    def load(q):
        src = x_hbm.at[q // per_panel, :, pl.ds((q % per_panel) * width, width)]
        return pltpu.make_async_copy(src, gathered.at[q, r], load_sem.at[q])

    def stage_copy(i):
        src = a_hbm.at[pl.ds(pl.multiple_of(i * tile, tile), tile)]
        return pltpu.make_async_copy(src, stage.at[i % 2], stage_sem.at[i % 2])

    def hop(q, block, h, way, target):
        ref = gathered.at[q, block, pl.ds(pl.multiple_of(h * half, half), half)]
        return pltpu.make_async_remote_copy(
            ref, ref, send_sem.at[way, q, block, h], recv_sem.at[q, block, h],
            device_id={"row": target}, device_id_type=MESH)

    def each_send(q, s, h, act):
        @pl.when((r + 1 < rows_axis) & (r - s >= 0))
        def _():
            act(hop(q, r - s, h, 0, r + 1))

        @pl.when((r >= 1) & (r + s < rows_axis))
        def _():
            act(hop(q, r + s, h, 1, r - 1))

    def wait_arrivals(q, s, h):
        @pl.when(r - 1 - s >= 0)
        def _():
            hop(q, r - 1 - s, h, 0, r - 1).wait_recv()

        @pl.when(r + 1 + s < rows_axis)
        def _():
            hop(q, r + 1 + s, h, 1, r + 1).wait_recv()

    def part(q, target, source):
        return pltpu.make_async_remote_copy(
            partial.at[q, target], received.at[q, source], part_send.at[q, target], part_recv.at[q, source],
            device_id={"col": target}, device_id_type=MESH)

    def own_copy(q, target):
        return pltpu.make_async_remote_copy(
            gathered.at[q, (r * cols_axis + target) % rows_axis], own.at[q], own_send.at[q, target], own_recv.at[q],
            device_id={"col": target}, device_id_type=MESH)

    def own_here(q):
        return pltpu.make_async_copy(gathered.at[q, (r * cols_axis + c) % rows_axis], own.at[q], own_local.at[q])

    own_root = (r * cols_axis + c) // rows_axis

    def each_own(q, act):
        for shift in range(1, cols_axis):
            target = (c + shift) % cols_axis

            @pl.when((r * cols_axis + target) // rows_axis == c)
            def _():
                act(own_copy(q, target))

    for q in range(chunks):
        load(q).start()
    stage_copy(0).start()
    barrier = pltpu.get_barrier_semaphore()
    for shift in range(1, cols_axis):
        pl.semaphore_signal(barrier, inc=1, device_id={"col": (c + shift) % cols_axis}, device_id_type=MESH)

    @pl.when(r >= 1)
    def _():
        pl.semaphore_signal(barrier, inc=1, device_id={"row": r - 1}, device_id_type=MESH)

    @pl.when(r + 1 < rows_axis)
    def _():
        pl.semaphore_signal(barrier, inc=1, device_id={"row": r + 1}, device_id_type=MESH)

    inner = (r >= 1) & (r + 1 < rows_axis)

    @pl.when(inner)
    def _():
        pl.semaphore_wait(barrier, cols_axis + 1)

    @pl.when(jnp.logical_not(inner))
    def _():
        pl.semaphore_wait(barrier, cols_axis)

    for q in range(chunks):
        load(q).wait()

    def split_tile(i, carry):
        @pl.when(i + 1 < tiles)
        def _():
            stage_copy(i + 1).start()

        stage_copy(i).wait()
        at = pl.ds(pl.multiple_of(i * tile, tile), tile)
        value = stage[i % 2]
        high = value.astype(jnp.bfloat16)
        a_hi[at, :] = high
        a_lo[at, :] = (value - high.astype(jnp.float32)).astype(jnp.bfloat16)
        return carry

    def multiply(k, i):
        even = 1 - 2 * (c % 2)
        target = (c + cols_axis // 2 + even * i + cols_axis) % cols_axis
        at = pl.ds(pl.multiple_of(target * rows, rows), rows)
        high = a_hi[at, :]
        out = jnp.dot(high, p_hi[...], preferred_element_type=jnp.float32)
        out += jnp.dot(high, p_lo[...], preferred_element_type=jnp.float32)
        out += jnp.dot(a_lo[at, :], p_hi[...], preferred_element_type=jnp.float32)
        partial[k, target] = out

        @pl.when(target != c)
        def _():
            part(k, target, c).start()

    def step(u, carry):
        q, p = u // pieces, u % pieces
        s, h = p // 2, p % 2

        @pl.when((u >= 2) & (u < chunks * pieces + 2))
        def _():
            v = u - 2
            wait_arrivals(v // pieces, (v % pieces) // 2, v % 2)

        @pl.when(q < chunks)
        def _():
            each_send(q, s, h, lambda copy: copy.start())

        @pl.when(u == 1)
        def _():
            lax.fori_loop(0, tiles, split_tile, 0)

        @pl.when((q >= 1) & (p == 1))
        def _():
            k = q - 1
            each_own(k, lambda copy: copy.start())

            @pl.when(own_root == c)
            def _():
                own_here(k).start()

            def split_panel(b, carry):
                at = pl.ds(pl.multiple_of(b * rows, rows), rows)
                value = gathered[k, b]
                high = value.astype(jnp.bfloat16)
                p_hi[at, :] = high
                p_lo[at, :] = (value - high.astype(jnp.float32)).astype(jnp.bfloat16)
                return carry

            lax.fori_loop(0, rows_axis, split_panel, 0)

        @pl.when((q >= 1) & (p >= 1))
        def _():
            def body(i, carry):
                multiply(q - 1, i)
                return carry

            lax.fori_loop((p - 1) * cols_axis // (pieces - 1), p * cols_axis // (pieces - 1), body, 0)

        return carry

    lax.fori_loop(0, (chunks + 1) * pieces, step, 0)

    for q in range(chunks):
        panel, start = q // per_panel, (q % per_panel) * width
        at = (panel, slice(None), slice(start, start + width))
        total = partial[q, c]
        for shift in range(1, cols_axis):
            source = (c + shift) % cols_axis
            part(q, source, source).wait_recv()
            total += received[q, source]
        y_ref[at] = total

        @pl.when(own_root == c)
        def _():
            own_here(q).wait()

        @pl.when(own_root != c)
        def _():
            own_copy(q, own_root).wait_recv()

        own_ref[at] = own[q]

    def drain(u, carry):
        q, p = u // pieces, u % pieces
        each_send(q, p // 2, p % 2, lambda copy: copy.wait_send())
        return carry

    lax.fori_loop(0, chunks * pieces, drain, 0)
    for q in range(chunks):
        each_own(q, lambda copy: copy.wait_send())
        for shift in range(1, cols_axis):
            part(q, (c + shift) % cols_axis, c).wait_send()


def products(inverse_tile, masked):
    rows_axis, cols_axis = lax.axis_size("row"), lax.axis_size("col")
    height, depth = inverse_tile.shape
    count, rows, columns = masked.shape
    width = min(256, columns)
    chunks = count * columns // width
    tile = min(128, height)
    f32, bf16 = jnp.float32, jnp.bfloat16
    dma = pltpu.SemaphoreType.DMA
    result = jax.ShapeDtypeStruct((count, rows, columns), f32)
    return pl.pallas_call(
        functools.partial(exchange, (rows_axis, cols_axis), chunks),
        out_shape=(result, result),
        in_specs=[pl.BlockSpec(memory_space=pl.ANY)] * 2,
        out_specs=[pl.BlockSpec(memory_space=pltpu.VMEM)] * 2,
        scratch_shapes=[
            pltpu.VMEM((height, depth), bf16),
            pltpu.VMEM((height, depth), bf16),
            pltpu.VMEM((2, tile, depth), f32),
            pltpu.VMEM((depth, width), bf16),
            pltpu.VMEM((depth, width), bf16),
            pltpu.VMEM((chunks, rows_axis, rows, width), f32),
            pltpu.VMEM((chunks, cols_axis, rows, width), f32),
            pltpu.VMEM((chunks, cols_axis, rows, width), f32),
            pltpu.VMEM((chunks, rows, width), f32),
            dma((2,)),
            dma((chunks,)),
            dma((2, chunks, rows_axis, 2)),
            dma((chunks, rows_axis, 2)),
            dma((chunks, cols_axis)),
            dma((chunks, cols_axis)),
            dma((chunks, cols_axis)),
            dma((chunks,)),
            dma((chunks,)),
        ],
        compiler_params=pltpu.CompilerParams(
            collective_id=0, has_side_effects=True, vmem_limit_bytes=60 * 1024 * 1024),
    )(inverse_tile, masked)


def finish(y, own, link, diag_inverse):
    row_id = lax.axis_index("row")
    col_id = lax.axis_index("col")
    height, span = diag_inverse.shape[1:]
    first, second = own[0], own[1]
    y1 = -y[0]
    y2 = -(y[1] + dot(y1, link, (1, 0)))
    shifted = second - dot(first, link, (1, 0))
    link_rows = lax.dynamic_slice_in_dim(link, row_id * height, height, 0)
    link_cols = lax.dynamic_slice_in_dim(link, col_id * span, span, 0)
    given = dot(diag_inverse[0], link_cols, (1, 0))
    f1 = dot(first, y1, (0, 0))
    f2 = dot(first, y2, (0, 0))
    f2 = lax.dynamic_update_slice_in_dim(
        f2, lax.dynamic_slice_in_dim(f2, row_id * height, height, 0) + given, row_id * height, 0
    )
    s2 = dot(shifted, y2, (0, 0)) - dot(link_rows, given, (0, 0))
    terms = jnp.stack([f1, f2, s2])
    terms = lax.psum_scatter(terms, "row", scatter_dimension=1, tiled=True)
    terms = lax.psum_scatter(terms, "col", scatter_dimension=2, tiled=True)
    diag = jnp.stack([diag_inverse[0] - terms[0], diag_inverse[1] - terms[2]])
    return jnp.stack([y1, y2]), diag, -terms[1]


def local(inverse_tile, panels, link_panel, diag_inverse, ancestor_tiles):
    masked = mask_panels(panels, ancestor_tiles)[0]
    ys, own = products(inverse_tile, masked)
    anc, diag, cross = finish(ys, own, link_panel[0], diag_inverse[0])
    return anc[None], diag[None], cross[None]


def solution(mesh):
    in_specs = (
        P(("hyp", "row"), "col"),
        P("hyp", None, ("col", "row"), None),
        P("hyp", None, None),
        P("hyp", None, "row", "col"),
        P(),
    )
    out_specs = (
        P("hyp", None, ("row", "col"), None),
        P("hyp", None, "row", "col"),
        P("hyp", "row", "col"),
    )
    return jax.shard_map(local, mesh=mesh, in_specs=in_specs, out_specs=out_specs, check_vma=False)
```

```python
import functools

import jax
import jax.numpy as jnp
from jax import lax
from jax.experimental import pallas as pl
from jax.experimental.pallas import tpu as pltpu
from jax.sharding import PartitionSpec as P

TILE = 128
MESH = pl.DeviceIdType.MESH

precise = lax.Precision.HIGH


def dot(a, b, contract, precision=precise):
    return lax.dot_general(a, b, ((contract[0:1], contract[1:2]), ((), ())), precision=precision)


def mask_panels(panels, ancestor_tiles):
    rows_axis = lax.axis_size("row")
    local_rows = panels.shape[2]
    row_start = (lax.axis_index("col") * rows_axis + lax.axis_index("row")) * local_rows
    tile_mask = jnp.repeat(ancestor_tiles, TILE, axis=2)
    kept_rows = lax.dynamic_slice_in_dim(tile_mask, row_start, local_rows, 2)
    return jnp.where(kept_rows[..., None] != 0, panels, 0.0)


def exchange(axis_sizes, chunks, a_hbm, x_hbm, y_ref, own_ref, a_hi, a_lo, stage, p_hi, p_lo, gathered, partial,
             received, own, stage_sem, load_sem, send_sem, recv_sem, part_send, part_recv, own_send, own_recv, own_local):
    rows_axis, cols_axis = axis_sizes
    r = lax.axis_index("row")
    c = lax.axis_index("col")
    _, _, rows, width = gathered.shape
    half = rows // 2
    per_panel = chunks // x_hbm.shape[0]
    pieces = 2 * (rows_axis - 1)
    tile = stage.shape[1]
    tiles = a_hbm.shape[0] // tile

    def load(q):
        src = x_hbm.at[q // per_panel, :, pl.ds((q % per_panel) * width, width)]
        return pltpu.make_async_copy(src, gathered.at[q, r], load_sem.at[q])

    def stage_copy(i):
        src = a_hbm.at[pl.ds(pl.multiple_of(i * tile, tile), tile)]
        return pltpu.make_async_copy(src, stage.at[i % 2], stage_sem.at[i % 2])

    def hop(q, block, h, way, target):
        ref = gathered.at[q, block, pl.ds(pl.multiple_of(h * half, half), half)]
        return pltpu.make_async_remote_copy(
            ref, ref, send_sem.at[way, q, block, h], recv_sem.at[q, block, h],
            device_id={"row": target}, device_id_type=MESH)

    def each_send(q, s, h, act):
        @pl.when((r + 1 < rows_axis) & (r - s >= 0))
        def _():
            act(hop(q, r - s, h, 0, r + 1))

        @pl.when((r >= 1) & (r + s < rows_axis))
        def _():
            act(hop(q, r + s, h, 1, r - 1))

    def wait_arrivals(q, s, h):
        @pl.when(r - 1 - s >= 0)
        def _():
            hop(q, r - 1 - s, h, 0, r - 1).wait_recv()

        @pl.when(r + 1 + s < rows_axis)
        def _():
            hop(q, r + 1 + s, h, 1, r + 1).wait_recv()

    def part(q, target, source):
        return pltpu.make_async_remote_copy(
            partial.at[q, target], received.at[q, source], part_send.at[q, target], part_recv.at[q, source],
            device_id={"col": target}, device_id_type=MESH)

    def own_copy(q, target):
        return pltpu.make_async_remote_copy(
            gathered.at[q, (r * cols_axis + target) % rows_axis], own.at[q], own_send.at[q, target], own_recv.at[q],
            device_id={"col": target}, device_id_type=MESH)

    def own_here(q):
        return pltpu.make_async_copy(gathered.at[q, (r * cols_axis + c) % rows_axis], own.at[q], own_local.at[q])

    own_root = (r * cols_axis + c) // rows_axis

    def each_own(q, act):
        for shift in range(1, cols_axis):
            target = (c + shift) % cols_axis

            @pl.when((r * cols_axis + target) // rows_axis == c)
            def _():
                act(own_copy(q, target))

    for q in range(chunks):
        load(q).start()
    stage_copy(0).start()
    barrier = pltpu.get_barrier_semaphore()
    for shift in range(1, cols_axis):
        pl.semaphore_signal(barrier, inc=1, device_id={"col": (c + shift) % cols_axis}, device_id_type=MESH)

    @pl.when(r >= 1)
    def _():
        pl.semaphore_signal(barrier, inc=1, device_id={"row": r - 1}, device_id_type=MESH)

    @pl.when(r + 1 < rows_axis)
    def _():
        pl.semaphore_signal(barrier, inc=1, device_id={"row": r + 1}, device_id_type=MESH)

    inner = (r >= 1) & (r + 1 < rows_axis)

    @pl.when(inner)
    def _():
        pl.semaphore_wait(barrier, cols_axis + 1)

    @pl.when(jnp.logical_not(inner))
    def _():
        pl.semaphore_wait(barrier, cols_axis)

    for q in range(chunks):
        load(q).wait()

    def split_tile(i, carry):
        @pl.when(i + 1 < tiles)
        def _():
            stage_copy(i + 1).start()

        stage_copy(i).wait()
        at = pl.ds(pl.multiple_of(i * tile, tile), tile)
        value = stage[i % 2]
        high = value.astype(jnp.bfloat16)
        a_hi[at, :] = high
        a_lo[at, :] = (value - high.astype(jnp.float32)).astype(jnp.bfloat16)
        return carry

    def multiply(k, i):
        even = 1 - 2 * (c % 2)
        target = (c + cols_axis // 2 + even * i + cols_axis) % cols_axis
        at = pl.ds(pl.multiple_of(target * rows, rows), rows)
        high = a_hi[at, :]
        out = jnp.dot(high, p_hi[...], preferred_element_type=jnp.float32)
        out += jnp.dot(high, p_lo[...], preferred_element_type=jnp.float32)
        out += jnp.dot(a_lo[at, :], p_hi[...], preferred_element_type=jnp.float32)
        partial[k, target] = out

        @pl.when(target != c)
        def _():
            part(k, target, c).start()

    def step(u, carry):
        q, p = u // pieces, u % pieces
        s, h = p // 2, p % 2

        @pl.when((u >= 2) & (u < chunks * pieces + 2))
        def _():
            v = u - 2
            wait_arrivals(v // pieces, (v % pieces) // 2, v % 2)

        @pl.when(q < chunks)
        def _():
            each_send(q, s, h, lambda copy: copy.start())

        @pl.when(u == 1)
        def _():
            lax.fori_loop(0, tiles, split_tile, 0)

        @pl.when((q >= 1) & (p == 1))
        def _():
            k = q - 1
            each_own(k, lambda copy: copy.start())

            @pl.when(own_root == c)
            def _():
                own_here(k).start()

            def split_panel(b, carry):
                at = pl.ds(pl.multiple_of(b * rows, rows), rows)
                value = gathered[k, b]
                high = value.astype(jnp.bfloat16)
                p_hi[at, :] = high
                p_lo[at, :] = (value - high.astype(jnp.float32)).astype(jnp.bfloat16)
                return carry

            lax.fori_loop(0, rows_axis, split_panel, 0)

        @pl.when((q >= 1) & (p >= 1))
        def _():
            def body(i, carry):
                multiply(q - 1, i)
                return carry

            lax.fori_loop((p - 1) * cols_axis // (pieces - 1), p * cols_axis // (pieces - 1), body, 0)

        return carry

    lax.fori_loop(0, (chunks + 1) * pieces, step, 0)

    for q in range(chunks):
        panel, start = q // per_panel, (q % per_panel) * width
        at = (panel, slice(None), slice(start, start + width))
        total = partial[q, c]
        for shift in range(1, cols_axis):
            source = (c + shift) % cols_axis
            part(q, source, source).wait_recv()
            total += received[q, source]
        y_ref[at] = total

        @pl.when(own_root == c)
        def _():
            own_here(q).wait()

        @pl.when(own_root != c)
        def _():
            own_copy(q, own_root).wait_recv()

        own_ref[at] = own[q]

    def drain(u, carry):
        q, p = u // pieces, u % pieces
        each_send(q, p // 2, p % 2, lambda copy: copy.wait_send())
        return carry

    lax.fori_loop(0, chunks * pieces, drain, 0)
    for q in range(chunks):
        each_own(q, lambda copy: copy.wait_send())
        for shift in range(1, cols_axis):
            part(q, (c + shift) % cols_axis, c).wait_send()


def products(inverse_tile, masked):
    rows_axis, cols_axis = lax.axis_size("row"), lax.axis_size("col")
    height, depth = inverse_tile.shape
    count, rows, columns = masked.shape
    width = min(256, columns)
    chunks = count * columns // width
    tile = min(128, height)
    f32, bf16 = jnp.float32, jnp.bfloat16
    dma = pltpu.SemaphoreType.DMA
    result = jax.ShapeDtypeStruct((count, rows, columns), f32)
    return pl.pallas_call(
        functools.partial(exchange, (rows_axis, cols_axis), chunks),
        out_shape=(result, result),
        in_specs=[pl.BlockSpec(memory_space=pl.ANY)] * 2,
        out_specs=[pl.BlockSpec(memory_space=pltpu.VMEM)] * 2,
        scratch_shapes=[
            pltpu.VMEM((height, depth), bf16),
            pltpu.VMEM((height, depth), bf16),
            pltpu.VMEM((2, tile, depth), f32),
            pltpu.VMEM((depth, width), bf16),
            pltpu.VMEM((depth, width), bf16),
            pltpu.VMEM((chunks, rows_axis, rows, width), f32),
            pltpu.VMEM((chunks, cols_axis, rows, width), f32),
            pltpu.VMEM((chunks, cols_axis, rows, width), f32),
            pltpu.VMEM((chunks, rows, width), f32),
            dma((2,)),
            dma((chunks,)),
            dma((2, chunks, rows_axis, 2)),
            dma((chunks, rows_axis, 2)),
            dma((chunks, cols_axis)),
            dma((chunks, cols_axis)),
            dma((chunks, cols_axis)),
            dma((chunks,)),
            dma((chunks,)),
        ],
        compiler_params=pltpu.CompilerParams(
            collective_id=0, has_side_effects=True, vmem_limit_bytes=60 * 1024 * 1024),
    )(inverse_tile, masked)


def halving_levels():
    levels = []
    for axis in ("col", "row"):
        dist = 1
        while dist < lax.axis_size(axis):
            levels.append((axis, dist))
            dist *= 2
    return levels


def halve(levels, count, terms, out_ref, *scratch):
    depth = len(levels)
    kept = (terms,) + scratch[: depth - 1]
    landed = scratch[depth - 1 : 2 * depth - 1]
    send_sem, recv_sem = scratch[2 * depth - 1 :]

    def bit_and_partner(level):
        axis, dist = levels[level]
        at = lax.axis_index(axis)
        bit = (at // dist) % 2
        return bit, {axis: at + dist * (1 - 2 * bit)}

    def copy(level, k):
        bit, partner = bit_and_partner(level)
        return pltpu.make_async_remote_copy(
            kept[level].at[k, :, 1 - bit], landed[level].at[k], send_sem.at[level, k], recv_sem.at[level, k],
            device_id=partner, device_id_type=MESH)

    barrier = pltpu.get_barrier_semaphore()
    for level in range(depth):
        pl.semaphore_signal(barrier, inc=1, device_id=bit_and_partner(level)[1], device_id_type=MESH)
    pl.semaphore_wait(barrier, depth)

    for level in range(depth + 1):
        for k in range(count):
            if level > 0:
                copy(level - 1, k).wait_recv()
                bit, _ = bit_and_partner(level - 1)
                total = kept[level - 1][k, :, bit] + landed[level - 1][k]
                target = kept[level] if level < depth else out_ref
                target[k] = total.reshape(target.shape[1:])
            if level < depth:
                copy(level, k).start()
    for level in range(depth):
        for k in range(count):
            copy(level, k).wait_send()


def reduce_blocks(terms, height, span):
    rows_axis, cols_axis = lax.axis_size("row"), lax.axis_size("col")
    count = terms.shape[0]
    terms = terms.reshape(count, rows_axis, height, cols_axis, span).transpose(0, 3, 1, 2, 4)
    levels = halving_levels()
    shapes = []
    cols, rows = cols_axis, rows_axis
    for axis, _ in levels:
        if axis == "col":
            cols //= 2
            shapes.append(((cols, 2, rows, height, span), (cols, rows, height, span)))
        else:
            rows //= 2
            shapes.append(((rows, 2, height, span), (rows, height, span)))
    dma = pltpu.SemaphoreType.DMA((len(levels), count))
    return pl.pallas_call(
        functools.partial(halve, levels, count),
        out_shape=jax.ShapeDtypeStruct((count, height, span), jnp.float32),
        in_specs=[pl.BlockSpec(memory_space=pltpu.VMEM)],
        out_specs=pl.BlockSpec(memory_space=pltpu.VMEM),
        scratch_shapes=[pltpu.VMEM((count,) + kept, jnp.float32) for kept, _ in shapes[1:]]
        + [pltpu.VMEM((count,) + landed, jnp.float32) for _, landed in shapes]
        + [dma, dma],
        compiler_params=pltpu.CompilerParams(
            collective_id=1, has_side_effects=True, vmem_limit_bytes=32 * 1024 * 1024),
    )(terms.reshape((count,) + shapes[0][0]))


def finish(y, own, link, diag_inverse):
    row_id = lax.axis_index("row")
    col_id = lax.axis_index("col")
    height, span = diag_inverse.shape[1:]
    first, second = own[0], own[1]
    y1 = -y[0]
    y2 = -(y[1] + dot(y1, link, (1, 0)))
    shifted = second - dot(first, link, (1, 0))
    link_rows = lax.dynamic_slice_in_dim(link, row_id * height, height, 0)
    link_cols = lax.dynamic_slice_in_dim(link, col_id * span, span, 0)
    given = dot(diag_inverse[0], link_cols, (1, 0))
    f1 = dot(first, y1, (0, 0))
    f2 = dot(first, y2, (0, 0))
    f2 = lax.dynamic_update_slice_in_dim(
        f2, lax.dynamic_slice_in_dim(f2, row_id * height, height, 0) + given, row_id * height, 0
    )
    s2 = dot(shifted, y2, (0, 0)) - dot(link_rows, given, (0, 0))
    terms = jnp.stack([f1, f2, s2])
    terms = reduce_blocks(terms, height, span)
    diag = jnp.stack([diag_inverse[0] - terms[0], diag_inverse[1] - terms[2]])
    return jnp.stack([y1, y2]), diag, -terms[1]


def local(inverse_tile, panels, link_panel, diag_inverse, ancestor_tiles):
    masked = mask_panels(panels, ancestor_tiles)[0]
    ys, own = products(inverse_tile, masked)
    anc, diag, cross = finish(ys, own, link_panel[0], diag_inverse[0])
    return anc[None], diag[None], cross[None]


def solution(mesh):
    in_specs = (
        P(("hyp", "row"), "col"),
        P("hyp", None, ("col", "row"), None),
        P("hyp", None, None),
        P("hyp", None, "row", "col"),
        P(),
    )
    out_specs = (
        P("hyp", None, ("row", "col"), None),
        P("hyp", None, "row", "col"),
        P("hyp", "row", "col"),
    )
    return jax.shard_map(local, mesh=mesh, in_specs=in_specs, out_specs=out_specs, check_vma=False)
```

```python
import functools

import jax
import jax.numpy as jnp
from jax import lax
from jax.experimental import pallas as pl
from jax.experimental.pallas import tpu as pltpu
from jax.sharding import PartitionSpec as P

TILE = 128
MESH = pl.DeviceIdType.MESH


def mask_panels(panels, ancestor_tiles):
    rows_axis = lax.axis_size("row")
    local_rows = panels.shape[2]
    row_start = (lax.axis_index("col") * rows_axis + lax.axis_index("row")) * local_rows
    tile_mask = jnp.repeat(ancestor_tiles, TILE, axis=2)
    kept_rows = lax.dynamic_slice_in_dim(tile_mask, row_start, local_rows, 2)
    return jnp.where(kept_rows[..., None] != 0, panels, 0.0)


def exchange(axis_sizes, chunks, a_hbm, x_hbm, y_ref, own_ref, a_hi, a_lo, stage, p_hi, p_lo, gathered, partial,
             received, own, stage_sem, load_sem, send_sem, recv_sem, part_send, part_recv, own_send, own_recv, own_local):
    rows_axis, cols_axis = axis_sizes
    r = lax.axis_index("row")
    c = lax.axis_index("col")
    _, _, rows, width = gathered.shape
    half = rows // 2
    per_panel = chunks // x_hbm.shape[0]
    pieces = 2 * (rows_axis - 1)
    tile = stage.shape[1]
    tiles = a_hbm.shape[0] // tile

    def load(q):
        src = x_hbm.at[q // per_panel, :, pl.ds((q % per_panel) * width, width)]
        return pltpu.make_async_copy(src, gathered.at[q, r], load_sem.at[q])

    def stage_copy(i):
        src = a_hbm.at[pl.ds(pl.multiple_of(i * tile, tile), tile)]
        return pltpu.make_async_copy(src, stage.at[i % 2], stage_sem.at[i % 2])

    def hop(q, block, h, way, target):
        ref = gathered.at[q, block, pl.ds(pl.multiple_of(h * half, half), half)]
        return pltpu.make_async_remote_copy(
            ref, ref, send_sem.at[way, q, block, h], recv_sem.at[q, block, h],
            device_id={"row": target}, device_id_type=MESH)

    def each_send(q, s, h, act):
        @pl.when((r + 1 < rows_axis) & (r - s >= 0))
        def _():
            act(hop(q, r - s, h, 0, r + 1))

        @pl.when((r >= 1) & (r + s < rows_axis))
        def _():
            act(hop(q, r + s, h, 1, r - 1))

    def wait_arrivals(q, s, h):
        @pl.when(r - 1 - s >= 0)
        def _():
            hop(q, r - 1 - s, h, 0, r - 1).wait_recv()

        @pl.when(r + 1 + s < rows_axis)
        def _():
            hop(q, r + 1 + s, h, 1, r + 1).wait_recv()

    def part(q, target, source):
        return pltpu.make_async_remote_copy(
            partial.at[q, target], received.at[q, source], part_send.at[q, target], part_recv.at[q, source],
            device_id={"col": target}, device_id_type=MESH)

    def own_copy(q, target):
        return pltpu.make_async_remote_copy(
            gathered.at[q, (r * cols_axis + target) % rows_axis], own.at[q], own_send.at[q, target], own_recv.at[q],
            device_id={"col": target}, device_id_type=MESH)

    def own_here(q):
        return pltpu.make_async_copy(gathered.at[q, (r * cols_axis + c) % rows_axis], own.at[q], own_local.at[q])

    own_root = (r * cols_axis + c) // rows_axis

    def each_own(q, act):
        for shift in range(1, cols_axis):
            target = (c + shift) % cols_axis

            @pl.when((r * cols_axis + target) // rows_axis == c)
            def _():
                act(own_copy(q, target))

    for q in range(chunks):
        load(q).start()
    stage_copy(0).start()
    barrier = pltpu.get_barrier_semaphore()
    for shift in range(1, cols_axis):
        pl.semaphore_signal(barrier, inc=1, device_id={"col": (c + shift) % cols_axis}, device_id_type=MESH)

    @pl.when(r >= 1)
    def _():
        pl.semaphore_signal(barrier, inc=1, device_id={"row": r - 1}, device_id_type=MESH)

    @pl.when(r + 1 < rows_axis)
    def _():
        pl.semaphore_signal(barrier, inc=1, device_id={"row": r + 1}, device_id_type=MESH)

    inner = (r >= 1) & (r + 1 < rows_axis)

    @pl.when(inner)
    def _():
        pl.semaphore_wait(barrier, cols_axis + 1)

    @pl.when(jnp.logical_not(inner))
    def _():
        pl.semaphore_wait(barrier, cols_axis)

    for q in range(chunks):
        load(q).wait()

    def split_tile(i, carry):
        @pl.when(i + 1 < tiles)
        def _():
            stage_copy(i + 1).start()

        stage_copy(i).wait()
        at = pl.ds(pl.multiple_of(i * tile, tile), tile)
        value = stage[i % 2]
        high = value.astype(jnp.bfloat16)
        a_hi[at, :] = high
        a_lo[at, :] = (value - high.astype(jnp.float32)).astype(jnp.bfloat16)
        return carry

    def multiply(k, i):
        even = 1 - 2 * (c % 2)
        target = (c + cols_axis // 2 + even * i + cols_axis) % cols_axis
        at = pl.ds(pl.multiple_of(target * rows, rows), rows)
        high = a_hi[at, :]
        out = jnp.dot(high, p_hi[...], preferred_element_type=jnp.float32)
        out += jnp.dot(high, p_lo[...], preferred_element_type=jnp.float32)
        out += jnp.dot(a_lo[at, :], p_hi[...], preferred_element_type=jnp.float32)
        partial[k, target] = out

        @pl.when(target != c)
        def _():
            part(k, target, c).start()

    def step(u, carry):
        q, p = u // pieces, u % pieces
        s, h = p // 2, p % 2

        @pl.when((u >= 2) & (u < chunks * pieces + 2))
        def _():
            v = u - 2
            wait_arrivals(v // pieces, (v % pieces) // 2, v % 2)

        @pl.when(q < chunks)
        def _():
            each_send(q, s, h, lambda copy: copy.start())

        @pl.when(u == 1)
        def _():
            lax.fori_loop(0, tiles, split_tile, 0)

        @pl.when((q >= 1) & (p == 1))
        def _():
            k = q - 1
            each_own(k, lambda copy: copy.start())

            @pl.when(own_root == c)
            def _():
                own_here(k).start()

            def split_panel(b, carry):
                at = pl.ds(pl.multiple_of(b * rows, rows), rows)
                value = gathered[k, b]
                high = value.astype(jnp.bfloat16)
                p_hi[at, :] = high
                p_lo[at, :] = (value - high.astype(jnp.float32)).astype(jnp.bfloat16)
                return carry

            lax.fori_loop(0, rows_axis, split_panel, 0)

        @pl.when((q >= 1) & (p >= 1))
        def _():
            def body(i, carry):
                multiply(q - 1, i)
                return carry

            lax.fori_loop((p - 1) * cols_axis // (pieces - 1), p * cols_axis // (pieces - 1), body, 0)

        return carry

    lax.fori_loop(0, (chunks + 1) * pieces, step, 0)

    for q in range(chunks):
        panel, start = q // per_panel, (q % per_panel) * width
        at = (panel, slice(None), slice(start, start + width))
        total = partial[q, c]
        for shift in range(1, cols_axis):
            source = (c + shift) % cols_axis
            part(q, source, source).wait_recv()
            total += received[q, source]
        y_ref[at] = total

        @pl.when(own_root == c)
        def _():
            own_here(q).wait()

        @pl.when(own_root != c)
        def _():
            own_copy(q, own_root).wait_recv()

        own_ref[at] = own[q]

    def drain(u, carry):
        q, p = u // pieces, u % pieces
        each_send(q, p // 2, p % 2, lambda copy: copy.wait_send())
        return carry

    lax.fori_loop(0, chunks * pieces, drain, 0)
    for q in range(chunks):
        each_own(q, lambda copy: copy.wait_send())
        for shift in range(1, cols_axis):
            part(q, (c + shift) % cols_axis, c).wait_send()


def products(inverse_tile, masked):
    rows_axis, cols_axis = lax.axis_size("row"), lax.axis_size("col")
    height, depth = inverse_tile.shape
    count, rows, columns = masked.shape
    width = min(256, columns)
    chunks = count * columns // width
    tile = min(128, height)
    f32, bf16 = jnp.float32, jnp.bfloat16
    dma = pltpu.SemaphoreType.DMA
    result = jax.ShapeDtypeStruct((count, rows, columns), f32)
    return pl.pallas_call(
        functools.partial(exchange, (rows_axis, cols_axis), chunks),
        out_shape=(result, result),
        in_specs=[pl.BlockSpec(memory_space=pl.ANY)] * 2,
        out_specs=[pl.BlockSpec(memory_space=pltpu.VMEM)] * 2,
        scratch_shapes=[
            pltpu.VMEM((height, depth), bf16),
            pltpu.VMEM((height, depth), bf16),
            pltpu.VMEM((2, tile, depth), f32),
            pltpu.VMEM((depth, width), bf16),
            pltpu.VMEM((depth, width), bf16),
            pltpu.VMEM((chunks, rows_axis, rows, width), f32),
            pltpu.VMEM((chunks, cols_axis, rows, width), f32),
            pltpu.VMEM((chunks, cols_axis, rows, width), f32),
            pltpu.VMEM((chunks, rows, width), f32),
            dma((2,)),
            dma((chunks,)),
            dma((2, chunks, rows_axis, 2)),
            dma((chunks, rows_axis, 2)),
            dma((chunks, cols_axis)),
            dma((chunks, cols_axis)),
            dma((chunks, cols_axis)),
            dma((chunks,)),
            dma((chunks,)),
        ],
        compiler_params=pltpu.CompilerParams(
            collective_id=0, has_side_effects=True, vmem_limit_bytes=60 * 1024 * 1024),
    )(inverse_tile, masked)


def halving_levels():
    levels = []
    for axis in ("col", "row"):
        dist = 1
        while dist < lax.axis_size(axis):
            levels.append((axis, dist))
            dist *= 2
    return levels


def split(value):
    high = value.astype(jnp.bfloat16)
    return high, (value - high.astype(jnp.float32)).astype(jnp.bfloat16)


def dot3(a, b, contract):
    def one(left, right):
        return lax.dot_general(
            left, right, (((contract,), (0,)), ((), ())), preferred_element_type=jnp.float32)

    return one(a[0], b[0]) + (one(a[0], b[1]) + one(a[1], b[0]))


def finish_kernel(levels, count, y_ref, own_ref, link_ref, given_ref, anc_ref, diag_ref, cross_ref, terms, out_ref, *scratch):
    depth = len(levels)
    height, span = given_ref.shape[1:]
    rows_axis, cols_axis = terms.shape[3], 2 * terms.shape[1]
    kept = (terms,) + scratch[: depth - 1]
    landed = scratch[depth - 1 : 2 * depth - 1]
    send_sem, recv_sem = scratch[2 * depth - 1 :]

    def bit_and_partner(level):
        axis, dist = levels[level]
        at = lax.axis_index(axis)
        bit = (at // dist) % 2
        return bit, {axis: at + dist * (1 - 2 * bit)}

    def copy(level, k):
        bit, partner = bit_and_partner(level)
        return pltpu.make_async_remote_copy(
            kept[level].at[k, :, 1 - bit], landed[level].at[k], send_sem.at[level, k], recv_sem.at[level, k],
            device_id=partner, device_id_type=MESH)

    barrier = pltpu.get_barrier_semaphore()
    for level in range(depth):
        pl.semaphore_signal(barrier, inc=1, device_id=bit_and_partner(level)[1], device_id_type=MESH)
    pl.semaphore_wait(barrier, depth)

    def store(k, value):
        for col in range(cols_axis):
            for row in range(rows_axis):
                terms[k, col // 2, col % 2, row] = value[
                    row * height : (row + 1) * height, col * span : (col + 1) * span]

    row_id, col_id = lax.axis_index("row"), lax.axis_index("col")
    y1 = -y_ref[0]
    anc_ref[0] = y1
    first, y1_parts = split(own_ref[0]), split(y1)
    store(0, dot3(first, y1_parts, 0))
    copy(0, 0).start()
    link = split(link_ref[...])
    link_cols = link_ref[pl.ds(pl.multiple_of(col_id * span, span), span), :]
    link_rows = link_ref[pl.ds(pl.multiple_of(row_id * height, height), height), :]
    given = dot3(split(given_ref[0]), split(link_cols), 1)
    y2 = -(y_ref[1] + dot3(y1_parts, link, 1))
    anc_ref[1] = y2
    y2_parts = split(y2)
    store(1, dot3(first, y2_parts, 0))
    for col in range(cols_axis):
        terms[1, col // 2, col % 2, row_id] += given[:, col * span : (col + 1) * span]
    copy(0, 1).start()
    shifted = split(own_ref[1] - dot3(first, link, 1))
    store(2, dot3(shifted, y2_parts, 0) - dot3(split(link_rows), split(given), 0))
    copy(0, 2).start()

    for level in range(1, depth + 1):
        for k in range(count):
            copy(level - 1, k).wait_recv()
            bit, _ = bit_and_partner(level - 1)
            total = kept[level - 1][k, :, bit] + landed[level - 1][k]
            target = kept[level] if level < depth else out_ref
            target[k] = total.reshape(target.shape[1:])
            if level < depth:
                copy(level, k).start()
    diag_ref[0] = given_ref[0] - out_ref[0]
    diag_ref[1] = given_ref[1] - out_ref[2]
    cross_ref[...] = -out_ref[1]
    for level in range(depth):
        for k in range(count):
            copy(level, k).wait_send()


def finish(y, own, link, given):
    rows_axis, cols_axis = lax.axis_size("row"), lax.axis_size("col")
    count = 3
    height, span = given.shape[1:]
    levels = halving_levels()
    shapes = []
    cols, rows = cols_axis, rows_axis
    for axis, _ in levels:
        if axis == "col":
            cols //= 2
            shapes.append(((cols, 2, rows, height, span), (cols, rows, height, span)))
        else:
            rows //= 2
            shapes.append(((rows, 2, height, span), (rows, height, span)))
    dma = pltpu.SemaphoreType.DMA((len(levels), count))
    return pl.pallas_call(
        functools.partial(finish_kernel, levels, count),
        out_shape=(
            jax.ShapeDtypeStruct(y.shape, jnp.float32),
            jax.ShapeDtypeStruct(given.shape, jnp.float32),
            jax.ShapeDtypeStruct((height, span), jnp.float32),
        ),
        in_specs=[pl.BlockSpec(memory_space=pltpu.VMEM)] * 4,
        out_specs=[pl.BlockSpec(memory_space=pltpu.VMEM)] * 3,
        scratch_shapes=[
            pltpu.VMEM((count,) + shapes[0][0], jnp.float32),
            pltpu.VMEM((count, height, span), jnp.float32),
        ]
        + [pltpu.VMEM((count,) + kept, jnp.float32) for kept, _ in shapes[1:]]
        + [pltpu.VMEM((count,) + landed, jnp.float32) for _, landed in shapes]
        + [dma, dma],
        compiler_params=pltpu.CompilerParams(
            collective_id=1, has_side_effects=True, vmem_limit_bytes=48 * 1024 * 1024),
    )(y, own, link, given)


def local(inverse_tile, panels, link_panel, diag_inverse, ancestor_tiles):
    masked = mask_panels(panels, ancestor_tiles)[0]
    ys, own = products(inverse_tile, masked)
    anc, diag, cross = finish(ys, own, link_panel[0], diag_inverse[0])
    return anc[None], diag[None], cross[None]


def solution(mesh):
    in_specs = (
        P(("hyp", "row"), "col"),
        P("hyp", None, ("col", "row"), None),
        P("hyp", None, None),
        P("hyp", None, "row", "col"),
        P(),
    )
    out_specs = (
        P("hyp", None, ("row", "col"), None),
        P("hyp", None, "row", "col"),
        P("hyp", "row", "col"),
    )
    return jax.shard_map(local, mesh=mesh, in_specs=in_specs, out_specs=out_specs, check_vma=False)
```
